32 devices in a mesh: comp: 2 (over y), lat: 4 (over x, core), lon: 4 (over z).
Axes of the slice: x: 2, y: 2, z: 4, core: 2. Of those that a mesh axis runs over, the one named last changes fastest.
Arguments:
- state: float32 [2, 3, 32, 64, 512], P('comp', None, None, 'lat', 'lon'), may hold values from -6 to 6
- wave_push: float32 [2, 32], P('comp'), may hold values from 0.2 to 0.6
- wave_fill: float32 [2, 32], P('comp'), may hold values from 0.2 to 0.6
- vertical: float32 [2, 32, 32], P('comp'), may hold values from -0.5 to 1
- land_mask: int32 [64, 512], P('lat', 'lon'), may hold values 0 or 1
- tile_match: int32 [4, 4, 2], P('lat'), may hold values from 0 to 3, as said below
- cell_counts: int32 [4, 4, 2], P('lat'), may hold values from 16 to 2032, as said below
Outputs:
- advanced: float32 [2, 3, 32, 64, 512], P('comp', None, None, 'lat', 'lon')
The draws below stay inside these ranges and needn't reach their ends.
Inputs may be any that keep to these rules, and one draw needn't show every extreme that they name: tile_match(i, j, 0) = j, and tile_match(i, j, 1) is j - 1 or j + 1 taken modulo 4. cell_counts(i, j, 0) + cell_counts(i, j, 1) = 2048, with both entries positive multiples of 16.
All inputs are finite; a program needn't handle non-finite values. No bound on the sum of `land_mask` on one device may be relied on, other than what follows from the above.
Results may differ from the reference program's by a relative error of at most 0.0001.
Values sent between devices are 32-bit elements; how exact they have to be, the bound alone decides.
A program may use at most 64 MiB of HBM per device.

```python
import math
import jax
import jax.numpy as jnp
from jax import lax

LEVELS = 32
FIELDS = 3
CLAT = 16
CLON = 128
TILES_LAT = 4
TILES_LON = 4
NLAT = 64
NLON = 512


def draw_vertical(key, part):
    key_off, key_diag = jax.random.split(jax.random.fold_in(key, 5))
    spread = 0.08
    offdiag = jnp.clip(jax.random.normal(key_off, (2, LEVELS, LEVELS), jnp.float32) * spread, -0.5, 0.5)
    diagonal = 0.8 + 0.2 * jax.random.uniform(key_diag, (2, LEVELS), jnp.float32)
    identity = jnp.eye(LEVELS, dtype=jnp.float32)
    return offdiag * (1.0 - identity) + diagonal[:, :, None] * identity


def draw_tile_match(key, part):
    side = jax.random.randint(jax.random.fold_in(key, 11), (TILES_LAT, TILES_LON), 0, 2).astype(jnp.int32) * 2 - 1
    columns = jnp.arange(TILES_LON).astype(jnp.int32)[None, :]
    first = jnp.broadcast_to(columns, (TILES_LAT, TILES_LON))
    second = (columns + side) % TILES_LON
    return jnp.stack([first, second.astype(jnp.int32)], axis=2).astype(jnp.int32)


def draw_cell_counts(key, part):
    shifted = jax.random.randint(jax.random.fold_in(key, 13), (TILES_LAT, TILES_LON), 1, CLON).astype(jnp.int32)
    row_ids = jnp.arange(TILES_LAT).astype(jnp.int32)[:, None]
    col_ids = jnp.arange(TILES_LON).astype(jnp.int32)[None, :]
    shifted = jnp.where((row_ids == 0) & (col_ids == 0), jnp.ones_like(shifted), shifted).astype(jnp.int32)
    shifted = jnp.where((row_ids == 0) & (col_ids == 1), jnp.full_like(shifted, CLON - 1), shifted).astype(jnp.int32)
    return jnp.stack([CLAT * (CLON - shifted), CLAT * shifted], axis=2).astype(jnp.int32)


def plant(entries, stream_key, least, largest):
    place = [jax.random.randint(jax.random.fold_in(stream_key, axis), (), 0, length) for axis, length in enumerate(entries.shape)]
    main_axis = entries.shape.index(max(entries.shape))
    beside = place[:main_axis] + [(place[main_axis] + 1) % entries.shape[main_axis]] + place[main_axis + 1:]
    return entries.at[tuple(place)].set(least).at[tuple(beside)].set(largest)


def block_scale(key, shape, shards, low, largest):
    gain = 1.0
    for dim, blocks in shards:
        heights = jax.random.uniform(jax.random.fold_in(jax.random.fold_in(key, 6), dim), (blocks,), jnp.float32, low / len(shards), largest / len(shards))
        gain = gain * jnp.repeat(jnp.exp(heights), shape[dim] // blocks).reshape((-1,) + (1,) * (len(shape) - 1 - dim))
    return gain


def centred(own_key, extent, scale, limit, cuts=(), held_as=jnp.bfloat16):
    drawn = jax.random.normal(own_key, extent, jnp.float32) * scale
    if len(cuts) > 0:
        drawn = block_scale(own_key, extent, cuts, -0.22, 0.18) * drawn
    return jnp.clip(drawn, min=-limit, max=limit).astype(held_as)


def setup_inputs(seed: int = 0) -> dict:
    splits = jax.random.split(jax.random.key(seed), 8)
    return {
        "state": centred(splits[0], (2, FIELDS, LEVELS, NLAT, NLON), 1.0, 6.0, ((0, 2), (3, 4), (4, 4)), jnp.float32),
        "wave_push": jnp.clip(jnp.exp(math.log(0.6) - 1.0986123 * jax.random.uniform(splits[1], (2, LEVELS), jnp.float32) ** block_scale(splits[1], (2, LEVELS), ((0, 2),), -0.2, 0.2)), 0.2, 0.6),
        "wave_fill": jnp.clip(jnp.exp(math.log(0.6) - 1.0986123 * jax.random.uniform(splits[2], (2, LEVELS), jnp.float32) ** block_scale(splits[2], (2, LEVELS), ((0, 2),), -0.2, 0.2)), 0.2, 0.6),
        "vertical": draw_vertical(jax.random.fold_in(splits[7], 71), 0),
        "land_mask": plant((jax.random.randint(splits[4], (NLAT, NLON), 0, 10) < 7).astype(jnp.int32), jax.random.fold_in(splits[4], 1), 0, 1),
        "tile_match": draw_tile_match(jax.random.fold_in(splits[7], 71), 0),
        "cell_counts": draw_cell_counts(jax.random.fold_in(splits[7], 71), 0),
    }


KAPPA = 0.5
CORIOLIS = 0.4


def diff_x(field):
    return (jnp.roll(field, -1, 3) - jnp.roll(field, 1, 3)) * 0.5


def diff_y(field):
    padded = jnp.pad(field, ((0, 0), (0, 0), (1, 1), (0, 0)))
    return (padded[:, :, 2:] - padded[:, :, :-2]) * 0.5


def substep(fields, push, fill, vertical, mask, fcor):
    u_old, v_old, p_old = fields[:, 0], fields[:, 1], fields[:, 2]
    u_one = u_old - push * diff_x(p_old) + fcor * v_old
    v_one = v_old - push * diff_y(p_old) - fcor * u_old
    div = diff_x(u_one) + diff_y(v_one)
    p_one = p_old - fill * div
    p_two = jnp.einsum('cam,cmyx->cayx', vertical, p_one, precision=lax.Precision.HIGHEST)
    return jnp.stack([u_one * mask, v_one * mask, p_two * mask], axis=1)


def reference(state, wave_push, wave_fill, vertical, land_mask, tile_match, cell_counts):
    mask = jnp.stack([jnp.ones((NLAT, NLON), jnp.float32), land_mask.astype(jnp.float32)])[:, None]
    rows = jnp.arange(NLAT).astype(jnp.float32)
    fcor = (CORIOLIS * jnp.sin(math.pi * ((rows + 0.5) / NLAT - 0.5)))[None, None, :, None]
    push = wave_push[:, :, None, None]
    fill = wave_fill[:, :, None, None]
    surface = state[:, :, 0]
    fields = state
    for step in range(2):
        fields = substep(fields, push, fill, vertical, mask, fcor)
    tiles = surface.reshape(2, FIELDS, TILES_LAT, CLAT, TILES_LON, CLON).transpose(0, 1, 2, 4, 3, 5)
    ids = jnp.arange(TILES_LON).astype(jnp.int32)
    hits = (tile_match[:, :, :, None] == ids[None, None, None, :]).astype(jnp.float32)
    weight = jnp.sum(hits * cell_counts.astype(jnp.float32)[:, :, :, None], axis=2)
    to_ocean = jnp.einsum('ijt,fitpq->fijpq', weight, tiles[0], precision=lax.Precision.HIGHEST)
    to_ocean = to_ocean / jnp.sum(weight, axis=2)[None, :, :, None, None]
    to_atmos = jnp.einsum('ijt,fijpq->fitpq', weight, tiles[1], precision=lax.Precision.HIGHEST)
    to_atmos = to_atmos / jnp.sum(weight, axis=1)[None, :, :, None, None]
    remapped = jnp.stack([to_atmos, to_ocean]).transpose(0, 1, 2, 4, 3, 5).reshape(2, FIELDS, NLAT, NLON)
    flux = KAPPA * (remapped - surface) * mask
    top = fields[:, :, 0] + flux
    return jnp.concatenate([top[:, :, None], fields[:, :, 1:]], axis=2)
```

```python
import functools
import math

import jax
import jax.numpy as jnp
from jax import lax
from jax.experimental import pallas as pl
from jax.experimental.pallas import tpu as pltpu
from jax.sharding import PartitionSpec as P

KAPPA = 0.5
CORIOLIS = 0.4
MESH = pl.DeviceIdType.MESH
STEPS = 2


def kernel(
    sizes,
    state,
    push_in,
    fill_in,
    vert_in,
    land_in,
    match_in,
    count_in,
    out,
    raw,
    push_v,
    fill_v,
    vert_v,
    land_v,
    match_v,
    count_v,
    pres,
    uone,
    vone,
    pone,
    unew,
    vnew,
    pack,
    from_lo,
    from_hi,
    edge,
    row_lo,
    row_hi,
    surf,
    load_sem,
    send_sem,
    recv_sem,
):
    levels, rows, cols, n_lat, n_lon = sizes
    comp = lax.axis_index("comp")
    lat = lax.axis_index("lat")
    lon = lax.axis_index("lon")
    west = lax.rem(lon + n_lon - 1, n_lon)
    east = lax.rem(lon + 1, n_lon)
    south = lax.rem(lat + n_lat - 1, n_lat)
    north = lax.rem(lat + 1, n_lat)
    other = 1 - comp
    plane = levels * rows

    barrier = pltpu.get_barrier_semaphore()
    for to in (
        (comp, lat, west),
        (comp, lat, east),
        (comp, south, lon),
        (comp, north, lon),
        (other, lat, lon),
        (other, lat, west),
        (other, lat, east),
    ):
        pl.semaphore_signal(barrier, inc=1, device_id=to, device_id_type=MESH)

    loads = []
    for f in (2, 0, 1):
        loads.append(
            pltpu.make_async_copy(
                state.at[pl.ds(f * plane, plane)],
                raw.at[pl.ds(f * plane, plane)],
                load_sem.at[f],
            )
        )
    for k, (src, dst) in enumerate(
        (
            (push_in, push_v),
            (fill_in, fill_v),
            (vert_in, vert_v),
            (land_in, land_v),
            (match_in, match_v),
            (count_in, count_v),
        )
    ):
        loads.append(pltpu.make_async_copy(src, dst, load_sem.at[3 + k]))
    for copy in loads:
        copy.start()

    lane = lax.broadcasted_iota(jnp.int32, (levels, cols), 1)
    first = lane == 0
    last = lane == cols - 1
    quad = lax.rem(lane, 4)
    row_id = lax.broadcasted_iota(jnp.int32, (rows, cols), 0) + lat * rows
    angle = (row_id.astype(jnp.float32) + 0.5) / (n_lat * rows) - 0.5
    fcor = CORIOLIS * jnp.sin(math.pi * angle)
    has_south = (lat > 0).astype(jnp.float32)
    has_north = (lat < n_lat - 1).astype(jnp.float32)

    for copy in loads:
        copy.wait()

    diag = lax.broadcasted_iota(jnp.int32, (levels, levels), 0) == lax.broadcasted_iota(
        jnp.int32, (levels, levels), 1
    )

    def per_level(ref):
        wide = jnp.broadcast_to(ref[...], (levels, levels))
        column = jnp.sum(jnp.where(diag, wide, 0.0), axis=1, keepdims=True)
        return jnp.broadcast_to(column * 0.5, (levels, cols))

    hp = per_level(push_v)
    hf = per_level(fill_v)
    vert = vert_v[...]
    vert_hi = vert.astype(jnp.bfloat16).astype(jnp.float32)
    vert_cat = jnp.concatenate([vert_hi, vert_hi, vert - vert_hi], axis=1).astype(
        jnp.bfloat16
    )
    mask = jnp.where(comp == 1, land_v[...].astype(jnp.float32), 1.0)

    def level_rows(y):
        return pl.ds(y, levels, stride=rows)

    def back(x):
        return jnp.where(first, 0.0, pltpu.roll(x, 1, 1))

    def ahead(x):
        return jnp.where(last, 0.0, pltpu.roll(x, cols - 1, 1))

    def remote(src, dst, k, to):
        return pltpu.make_async_remote_copy(
            src_ref=src,
            dst_ref=dst,
            send_sem=send_sem.at[k],
            recv_sem=recv_sem.at[k],
            device_id=to,
            device_id_type=MESH,
        )

    sends = []
    surf_sends = []
    for step in range(STEPS):
        base = 3 + 4 * step

        def get(f, y):
            if step == 0:
                return raw[pl.ds(f * plane + y, levels, stride=rows), :]
            return (unew, vnew, pres)[f][y]

        packed = jnp.zeros((levels, cols), jnp.float32)
        for y in range(rows):
            p = get(2, y)
            if step == 0:
                pres[y] = p
            u1 = get(0, y) + fcor[y : y + 1] * get(1, y) - hp * (ahead(p) - back(p))
            uone[y] = u1
            at = 4 * y + 2
            here = (lane == at) | (lane == at - 1)
            packed = jnp.where(here, pltpu.roll(p, at, 1), packed)
            at = 4 * (rows + y) + 2
            here = (lane == at) | (lane == at - 1)
            packed = jnp.where(here, pltpu.roll(u1, at, 1), packed)
        pack[step] = packed
        for y in (0, rows - 1):
            v1 = get(1, y) - fcor[y : y + 1] * get(0, y)
            v1 = v1 - hp * pres[y + 1] if y == 0 else v1 + hp * pres[y - 1]
            vone[y] = v1
            k = 0 if y == 0 else 1
            edge[step, k, 0] = pres[y]
            edge[step, k, 1] = v1
        if step == 0:
            pl.semaphore_wait(barrier, 7)
        lo = remote(pack.at[step], from_lo.at[step], base, (comp, lat, east))
        hi = remote(pack.at[step], from_hi.at[step], base + 1, (comp, lat, west))
        down = remote(edge.at[step, 0], row_hi.at[step], base + 2, (comp, south, lon))
        up = remote(edge.at[step, 1], row_lo.at[step], base + 3, (comp, north, lon))
        for copy in (lo, hi, down, up):
            copy.start()
            sends.append(copy)
        if step == 0:
            for k, to in enumerate((lon, east, west)):
                for f in range(3):
                    copy = remote(
                        raw.at[pl.ds(f * plane, rows)],
                        surf.at[k, f],
                        3 + 4 * STEPS + 3 * k + f,
                        (other, lat, to),
                    )
                    copy.start()
                    surf_sends.append(copy)

        for y in range(1, rows - 1):
            vone[y] = (
                get(1, y) - fcor[y : y + 1] * get(0, y) - hp * (pres[y + 1] - pres[y - 1])
            )
        for y in range(rows):
            u1 = uone[y]
            div = ahead(u1) - back(u1)
            if y + 1 < rows:
                div = div + vone[y + 1]
            if y > 0:
                div = div - vone[y - 1]
            pone[y] = pres[y] - hf * div

        down.wait_recv()
        up.wait_recv()
        p_lo = has_south * row_lo[step, 0]
        p_hi = has_north * row_hi[step, 0]
        v_lo = has_south * (row_lo[step, 1] - hp * pres[0])
        v_hi = has_north * (row_hi[step, 1] + hp * pres[rows - 1])
        fix_lo = hp * p_lo
        fix_hi = -hp * p_hi
        vone[0] = vone[0] + fix_lo
        vone[rows - 1] = vone[rows - 1] + fix_hi
        pone[0] = pone[0] + hf * v_lo
        pone[1] = pone[1] + hf * fix_lo
        pone[rows - 1] = pone[rows - 1] - hf * v_hi
        pone[rows - 2] = pone[rows - 2] - hf * fix_hi

        lo.wait_recv()
        hi.wait_recv()
        moved = jnp.where(
            quad == 1,
            pltpu.roll(from_hi[step], cols - 1, 1),
            pltpu.roll(from_lo[step], 1, 1),
        )
        signed = jnp.where(quad == 1, hp, -hp)
        u_side = pltpu.roll(moved, cols - 4 * rows, 1) + signed * packed
        u_fix = -signed * moved
        d_fix = jnp.where(
            quad == 1,
            u_side,
            jnp.where(
                quad == 2,
                -u_side,
                jnp.where(
                    quad == 0, pltpu.roll(u_fix, cols - 1, 1), -pltpu.roll(u_fix, 1, 1)
                ),
            ),
        )
        d_fix = hf * d_fix
        ends = first | last
        near = (lane < 2) | (lane > cols - 3)
        pieces = []
        for y in range(rows):
            turn = cols - (4 * y + 2)
            uone[y] = uone[y] + jnp.where(ends, pltpu.roll(u_fix, turn, 1), 0.0)
            p1 = pone[y] - jnp.where(near, pltpu.roll(d_fix, turn, 1), 0.0)
            p1_hi = p1.astype(jnp.bfloat16)
            p1_lo = (p1 - p1_hi.astype(jnp.float32)).astype(jnp.bfloat16)
            pieces.append(jnp.concatenate([p1_hi, p1_lo, p1_hi], axis=0))
        p2 = jnp.dot(
            vert_cat, jnp.concatenate(pieces, axis=1), preferred_element_type=jnp.float32
        )
        for y in range(rows):
            keep = mask[y : y + 1]
            u2 = keep * uone[y]
            v2 = keep * vone[y]
            pn = keep * p2[:, y * cols : (y + 1) * cols]
            if step + 1 < STEPS:
                unew[y] = u2
                vnew[y] = v2
                pres[y] = pn
            else:
                for f, value in enumerate((u2, v2, pn)):
                    out[pl.ds(f * plane + y, levels, stride=rows), :] = value

    count = count_v[...].astype(jnp.float32)
    match = match_v[...]
    tile = lax.broadcasted_iota(jnp.int32, match.shape, 0)

    def coef(peer):
        own = jnp.where((tile == lon) & (match == peer), count, 0.0)
        theirs = jnp.where((tile == peer) & (match == lon), count, 0.0)
        picked = jnp.where(comp == 1, own, theirs)
        total = jnp.sum(jnp.sum(picked, axis=1, keepdims=True), axis=0, keepdims=True)
        return jnp.broadcast_to(total, (rows, cols))

    coefs = [coef(lon), coef(west), coef(east)]
    inverse = KAPPA * mask / (coefs[0] + coefs[1] + coefs[2])
    scaled = [c * inverse for c in coefs]
    for copy in surf_sends:
        copy.wait_recv()
    for f in range(3):
        at = pl.ds(f * plane, rows)
        flux = -KAPPA * mask * raw[at]
        for k in range(3):
            flux = flux + scaled[k] * surf[k, f]
        out[at] = out[at] + flux
    for copy in sends + surf_sends:
        copy.wait_send()


def shards(n_lat, n_lon, state, push, fill, vertical, land, match, counts):
    _, fields, levels, rows, cols = state.shape
    assert fields == 3 and 8 * rows <= cols
    block = (rows, levels, cols)
    side = (STEPS, levels, cols)
    n_sems = 3 + 4 * STEPS + 9
    f32 = jnp.float32
    any_spec = pl.BlockSpec(memory_space=pl.ANY)
    result = pl.pallas_call(
        functools.partial(kernel, (levels, rows, cols, n_lat, n_lon)),
        out_shape=jax.ShapeDtypeStruct((fields * levels * rows, cols), f32),
        in_specs=[any_spec] * 7,
        out_specs=pl.BlockSpec(memory_space=pltpu.VMEM),
        scratch_shapes=[
            pltpu.VMEM((fields * levels * rows, cols), f32),
            pltpu.VMEM(push.shape, f32),
            pltpu.VMEM(fill.shape, f32),
            pltpu.VMEM(vertical.shape[1:], f32),
            pltpu.VMEM(land.shape, jnp.int32),
            pltpu.VMEM(match.shape[1:], jnp.int32),
            pltpu.VMEM(counts.shape[1:], jnp.int32),
            pltpu.VMEM(block, f32),
            pltpu.VMEM(block, f32),
            pltpu.VMEM(block, f32),
            pltpu.VMEM(block, f32),
            pltpu.VMEM(block, f32),
            pltpu.VMEM(block, f32),
            pltpu.VMEM(side, f32),
            pltpu.VMEM(side, f32),
            pltpu.VMEM(side, f32),
            pltpu.VMEM((STEPS, 2, 2, levels, cols), f32),
            pltpu.VMEM((STEPS, 2, levels, cols), f32),
            pltpu.VMEM((STEPS, 2, levels, cols), f32),
            pltpu.VMEM((3, fields, rows, cols), f32),
            pltpu.SemaphoreType.DMA((9,)),
            pltpu.SemaphoreType.DMA((n_sems,)),
            pltpu.SemaphoreType.DMA((n_sems,)),
        ],
        compiler_params=pltpu.CompilerParams(collective_id=0, has_side_effects=True),
        name="window",
    )(
        state.reshape(fields * levels * rows, cols),
        push,
        fill,
        vertical.reshape(vertical.shape[1:]),
        land,
        match.reshape(match.shape[1:]),
        counts.reshape(counts.shape[1:]),
    )
    return result.reshape(state.shape)


def solution(mesh):
    sizes = dict(mesh.shape)
    return jax.shard_map(
        functools.partial(shards, sizes["lat"], sizes["lon"]),
        mesh=mesh,
        in_specs=(
            P("comp", None, None, "lat", "lon"),
            P("comp", None),
            P("comp", None),
            P("comp", None, None),
            P("lat", "lon"),
            P("lat", None, None),
            P("lat", None, None),
        ),
        out_specs=P("comp", None, None, "lat", "lon"),
        check_vma=False,
    )
```

```python
import functools
import math

import jax
import jax.numpy as jnp
from jax import lax
from jax.experimental import pallas as pl
from jax.experimental.pallas import tpu as pltpu
from jax.sharding import PartitionSpec as P

KAPPA = 0.5
CORIOLIS = 0.4
MESH = pl.DeviceIdType.MESH
STEPS = 2


def kernel(
    sizes,
    state,
    push_in,
    fill_in,
    vert_in,
    land_in,
    match_in,
    count_in,
    out,
    raw,
    push_v,
    fill_v,
    vert_v,
    land_v,
    match_v,
    count_v,
    pres,
    uone,
    vone,
    pone,
    unew,
    vnew,
    pack,
    from_lo,
    from_hi,
    edge,
    row_lo,
    row_hi,
    surf,
    load_sem,
    send_sem,
    recv_sem,
):
    levels, rows, cols, n_lat, n_lon = sizes
    comp = lax.axis_index("comp")
    lat = lax.axis_index("lat")
    lon = lax.axis_index("lon")
    west = lax.rem(lon + n_lon - 1, n_lon)
    east = lax.rem(lon + 1, n_lon)
    south = lax.rem(lat + n_lat - 1, n_lat)
    north = lax.rem(lat + 1, n_lat)
    other = 1 - comp
    plane = levels * rows

    barrier = pltpu.get_barrier_semaphore()
    for to in (
        (comp, lat, west),
        (comp, lat, east),
        (comp, south, lon),
        (comp, north, lon),
        (other, lat, lon),
        (other, lat, west),
        (other, lat, east),
    ):
        pl.semaphore_signal(barrier, inc=1, device_id=to, device_id_type=MESH)

    loads = []
    for f in (2, 0, 1):
        loads.append(
            pltpu.make_async_copy(
                state.at[pl.ds(f * plane, plane)],
                raw.at[pl.ds(f * plane, plane)],
                load_sem.at[f],
            )
        )
    for k, (src, dst) in enumerate(
        (
            (push_in, push_v),
            (fill_in, fill_v),
            (vert_in, vert_v),
            (land_in, land_v),
            (match_in, match_v),
            (count_in, count_v),
        )
    ):
        loads.append(pltpu.make_async_copy(src, dst, load_sem.at[3 + k]))
    for copy in loads:
        copy.start()

    lane = lax.broadcasted_iota(jnp.int32, (levels, cols), 1)
    first = lane == 0
    last = lane == cols - 1
    quad = lax.rem(lane, 4)
    row_id = lax.broadcasted_iota(jnp.int32, (rows, cols), 0) + lat * rows
    angle = (row_id.astype(jnp.float32) + 0.5) / (n_lat * rows) - 0.5
    fcor = CORIOLIS * jnp.sin(math.pi * angle)
    has_south = (lat > 0).astype(jnp.float32)
    has_north = (lat < n_lat - 1).astype(jnp.float32)

    for copy in loads:
        copy.wait()

    diag = lax.broadcasted_iota(jnp.int32, (levels, levels), 0) == lax.broadcasted_iota(
        jnp.int32, (levels, levels), 1
    )

    def per_level(ref):
        wide = jnp.broadcast_to(ref[...], (levels, levels))
        column = jnp.sum(jnp.where(diag, wide, 0.0), axis=1, keepdims=True)
        return jnp.broadcast_to(column * 0.5, (levels, cols))

    hp = per_level(push_v)
    hf = per_level(fill_v)
    vert = vert_v[...]
    vert_hi = vert.astype(jnp.bfloat16).astype(jnp.float32)
    vert_cat = jnp.concatenate([vert_hi, vert_hi, vert - vert_hi], axis=1).astype(
        jnp.bfloat16
    )
    mask = jnp.where(comp == 1, land_v[...].astype(jnp.float32), 1.0)

    def level_rows(y):
        return pl.ds(y, levels, stride=rows)

    def back(x):
        return jnp.where(first, 0.0, pltpu.roll(x, 1, 1))

    def ahead(x):
        return jnp.where(last, 0.0, pltpu.roll(x, cols - 1, 1))

    def remote(src, dst, k, to):
        return pltpu.make_async_remote_copy(
            src_ref=src,
            dst_ref=dst,
            send_sem=send_sem.at[k],
            recv_sem=recv_sem.at[k],
            device_id=to,
            device_id_type=MESH,
        )

    sends = []
    surf_sends = []
    for step in range(STEPS):
        base = 3 + 4 * step

        def get(f, y):
            if step == 0:
                return raw[pl.ds(f * plane + y, levels, stride=rows), :]
            return (unew, vnew, pres)[f][y]

        packed = jnp.zeros((levels, cols), jnp.float32)
        for y in range(rows):
            p = get(2, y)
            if step == 0:
                pres[y] = p
            u1 = get(0, y) + fcor[y : y + 1] * get(1, y) - hp * (ahead(p) - back(p))
            uone[y] = u1
            at = 4 * y + 2
            here = (lane == at) | (lane == at - 1)
            packed = jnp.where(here, pltpu.roll(p, at, 1), packed)
            at = 4 * (rows + y) + 2
            here = (lane == at) | (lane == at - 1)
            packed = jnp.where(here, pltpu.roll(u1, at, 1), packed)
        pack[step] = packed
        for y in (0, rows - 1):
            v1 = get(1, y) - fcor[y : y + 1] * get(0, y)
            v1 = v1 - hp * pres[y + 1] if y == 0 else v1 + hp * pres[y - 1]
            vone[y] = v1
            k = 0 if y == 0 else 1
            edge[step, k, 0] = pres[y]
            edge[step, k, 1] = v1
        if step == 0:
            pl.semaphore_wait(barrier, 7)
        lo = remote(pack.at[step], from_lo.at[step], base, (comp, lat, east))
        hi = remote(pack.at[step], from_hi.at[step], base + 1, (comp, lat, west))
        down = remote(edge.at[step, 0], row_hi.at[step], base + 2, (comp, south, lon))
        up = remote(edge.at[step, 1], row_lo.at[step], base + 3, (comp, north, lon))
        for copy in (lo, hi, down, up):
            copy.start()
            sends.append(copy)
        if step == 0:
            for k, to in enumerate((lon, east, west)):
                for f in range(3):
                    copy = remote(
                        raw.at[pl.ds(f * plane, rows)],
                        surf.at[k, f],
                        3 + 4 * STEPS + 3 * k + f,
                        (other, lat, to),
                    )
                    copy.start()
                    surf_sends.append(copy)

        for y in range(1, rows - 1):
            vone[y] = (
                get(1, y) - fcor[y : y + 1] * get(0, y) - hp * (pres[y + 1] - pres[y - 1])
            )
        for y in range(rows):
            u1 = uone[y]
            div = ahead(u1) - back(u1)
            if y + 1 < rows:
                div = div + vone[y + 1]
            if y > 0:
                div = div - vone[y - 1]
            pone[y] = pres[y] - hf * div

        down.wait_recv()
        up.wait_recv()
        p_lo = has_south * row_lo[step, 0]
        p_hi = has_north * row_hi[step, 0]
        v_lo = has_south * (row_lo[step, 1] - hp * pres[0])
        v_hi = has_north * (row_hi[step, 1] + hp * pres[rows - 1])
        fix_lo = hp * p_lo
        fix_hi = -hp * p_hi
        vone[0] = vone[0] + fix_lo
        vone[rows - 1] = vone[rows - 1] + fix_hi
        pone[0] = pone[0] + hf * v_lo
        pone[1] = pone[1] + hf * fix_lo
        pone[rows - 1] = pone[rows - 1] - hf * v_hi
        pone[rows - 2] = pone[rows - 2] - hf * fix_hi

        lo.wait_recv()
        hi.wait_recv()
        moved = jnp.where(
            quad == 1,
            pltpu.roll(from_hi[step], cols - 1, 1),
            pltpu.roll(from_lo[step], 1, 1),
        )
        signed = jnp.where(quad == 1, hp, -hp)
        u_side = pltpu.roll(moved, cols - 4 * rows, 1) + signed * packed
        u_fix = -signed * moved
        d_fix = jnp.where(
            quad == 1,
            u_side,
            jnp.where(
                quad == 2,
                -u_side,
                jnp.where(
                    quad == 0, pltpu.roll(u_fix, cols - 1, 1), -pltpu.roll(u_fix, 1, 1)
                ),
            ),
        )
        d_fix = hf * d_fix
        ends = first | last
        near = (lane < 2) | (lane > cols - 3)
        pieces = []
        for y in range(rows):
            turn = cols - (4 * y + 2)
            uone[y] = uone[y] + jnp.where(ends, pltpu.roll(u_fix, turn, 1), 0.0)
            p1 = pone[y] - jnp.where(near, pltpu.roll(d_fix, turn, 1), 0.0)
            p1_hi = p1.astype(jnp.bfloat16)
            p1_lo = (p1 - p1_hi.astype(jnp.float32)).astype(jnp.bfloat16)
            pieces.append(jnp.concatenate([p1_hi, p1_lo, p1_hi], axis=0))
        p2 = jnp.dot(
            vert_cat, jnp.concatenate(pieces, axis=1), preferred_element_type=jnp.float32
        )
        for y in range(rows):
            keep = mask[y : y + 1]
            u2 = keep * uone[y]
            v2 = keep * vone[y]
            pn = keep * p2[:, y * cols : (y + 1) * cols]
            if step + 1 < STEPS:
                unew[y] = u2
                vnew[y] = v2
                pres[y] = pn
            else:
                for f, value in enumerate((u2, v2, pn)):
                    out[pl.ds(f * plane + y, levels, stride=rows), :] = value

    count = count_v[...].astype(jnp.float32)
    match = match_v[...]
    tile = lax.broadcasted_iota(jnp.int32, match.shape, 1)

    def coef(peer):
        own = jnp.where((tile == lon) & (match == peer), count, 0.0)
        theirs = jnp.where((tile == peer) & (match == lon), count, 0.0)
        picked = jnp.where(comp == 1, own, theirs)
        total = jnp.sum(jnp.sum(picked, axis=1, keepdims=True), axis=0, keepdims=True)
        return jnp.broadcast_to(total, (rows, cols))

    coefs = [coef(lon), coef(west), coef(east)]
    inverse = KAPPA * mask / (coefs[0] + coefs[1] + coefs[2])
    scaled = [c * inverse for c in coefs]
    for copy in surf_sends:
        copy.wait_recv()
    for f in range(3):
        at = pl.ds(f * plane, rows)
        flux = -KAPPA * mask * raw[at]
        for k in range(3):
            flux = flux + scaled[k] * surf[k, f]
        out[at] = out[at] + flux
    for copy in sends + surf_sends:
        copy.wait_send()


def shards(n_lat, n_lon, state, push, fill, vertical, land, match, counts):
    _, fields, levels, rows, cols = state.shape
    assert fields == 3 and 8 * rows <= cols
    block = (rows, levels, cols)
    side = (STEPS, levels, cols)
    n_sems = 3 + 4 * STEPS + 9
    f32 = jnp.float32
    any_spec = pl.BlockSpec(memory_space=pl.ANY)
    result = pl.pallas_call(
        functools.partial(kernel, (levels, rows, cols, n_lat, n_lon)),
        out_shape=pltpu.VMEM((fields * levels * rows, cols), f32),
        in_specs=[any_spec] * 7,
        out_specs=pl.BlockSpec(memory_space=pltpu.VMEM),
        scratch_shapes=[
            pltpu.VMEM((fields * levels * rows, cols), f32),
            pltpu.VMEM(push.shape, f32),
            pltpu.VMEM(fill.shape, f32),
            pltpu.VMEM(vertical.shape[1:], f32),
            pltpu.VMEM(land.shape, jnp.int32),
            pltpu.VMEM(match.shape[:0:-1], jnp.int32),
            pltpu.VMEM(counts.shape[:0:-1], jnp.int32),
            pltpu.VMEM(block, f32),
            pltpu.VMEM(block, f32),
            pltpu.VMEM(block, f32),
            pltpu.VMEM(block, f32),
            pltpu.VMEM(block, f32),
            pltpu.VMEM(block, f32),
            pltpu.VMEM(side, f32),
            pltpu.VMEM(side, f32),
            pltpu.VMEM(side, f32),
            pltpu.VMEM((STEPS, 2, 2, levels, cols), f32),
            pltpu.VMEM((STEPS, 2, levels, cols), f32),
            pltpu.VMEM((STEPS, 2, levels, cols), f32),
            pltpu.VMEM((3, fields, rows, cols), f32),
            pltpu.SemaphoreType.DMA((9,)),
            pltpu.SemaphoreType.DMA((n_sems,)),
            pltpu.SemaphoreType.DMA((n_sems,)),
        ],
        compiler_params=pltpu.CompilerParams(collective_id=0, has_side_effects=True),
        name="window",
    )(
        state.reshape(fields * levels * rows, cols),
        push,
        fill,
        vertical.reshape(vertical.shape[1:]),
        land,
        match[0].T,
        counts[0].T,
    )
    return result.reshape(state.shape)


def solution(mesh):
    sizes = dict(mesh.shape)
    return jax.shard_map(
        functools.partial(shards, sizes["lat"], sizes["lon"]),
        mesh=mesh,
        in_specs=(
            P("comp", None, None, "lat", "lon"),
            P("comp", None),
            P("comp", None),
            P("comp", None, None),
            P("lat", "lon"),
            P("lat", None, None),
            P("lat", None, None),
        ),
        out_specs=P("comp", None, None, "lat", "lon"),
        check_vma=False,
    )
```

```python
import functools
import math

import jax
import jax.numpy as jnp
from jax import lax
from jax.experimental import pallas as pl
from jax.experimental.pallas import tpu as pltpu
from jax.sharding import PartitionSpec as P

KAPPA = 0.5
CORIOLIS = 0.4
MESH = pl.DeviceIdType.MESH
STEPS = 2


def kernel(
    sizes,
    state,
    push_in,
    fill_in,
    vert_in,
    land_in,
    match_in,
    count_in,
    out,
    raw,
    push_v,
    fill_v,
    vert_v,
    land_v,
    match_v,
    count_v,
    pres,
    uone,
    vone,
    pone,
    unew,
    vnew,
    pack,
    from_lo,
    from_hi,
    edge,
    row_lo,
    row_hi,
    surf,
    load_sem,
    send_sem,
    recv_sem,
):
    levels, rows, cols, n_lat, n_lon = sizes
    comp = lax.axis_index("comp")
    lat = lax.axis_index("lat")
    lon = lax.axis_index("lon")
    west = lax.rem(lon + n_lon - 1, n_lon)
    east = lax.rem(lon + 1, n_lon)
    south = lax.rem(lat + n_lat - 1, n_lat)
    north = lax.rem(lat + 1, n_lat)
    other = 1 - comp
    plane = levels * rows

    barrier = pltpu.get_barrier_semaphore()
    for to in (
        (comp, lat, west),
        (comp, lat, east),
        (comp, south, lon),
        (comp, north, lon),
        (other, lat, lon),
        (other, lat, west),
        (other, lat, east),
    ):
        pl.semaphore_signal(barrier, inc=1, device_id=to, device_id_type=MESH)

    loads = []
    for f in (2, 0, 1):
        loads.append(
            pltpu.make_async_copy(
                state.at[pl.ds(f * plane, plane)],
                raw.at[pl.ds(f * plane, plane)],
                load_sem.at[f],
            )
        )
    for k, (src, dst) in enumerate(
        (
            (push_in, push_v),
            (fill_in, fill_v),
            (vert_in, vert_v),
            (land_in, land_v),
            (match_in, match_v),
            (count_in, count_v),
        )
    ):
        loads.append(pltpu.make_async_copy(src, dst, load_sem.at[3 + k]))
    for copy in loads:
        copy.start()

    lane = lax.broadcasted_iota(jnp.int32, (levels, cols), 1)
    first = lane == 0
    last = lane == cols - 1
    quad = lax.rem(lane, 4)
    row_id = lax.broadcasted_iota(jnp.int32, (rows, cols), 0) + lat * rows
    angle = (row_id.astype(jnp.float32) + 0.5) / (n_lat * rows) - 0.5
    fcor = CORIOLIS * jnp.sin(math.pi * angle)
    has_south = (lat > 0).astype(jnp.float32)
    has_north = (lat < n_lat - 1).astype(jnp.float32)

    for copy in loads:
        copy.wait()

    diag = lax.broadcasted_iota(jnp.int32, (levels, levels), 0) == lax.broadcasted_iota(
        jnp.int32, (levels, levels), 1
    )

    def per_level(ref):
        wide = jnp.broadcast_to(ref[...], (levels, levels))
        column = jnp.sum(jnp.where(diag, wide, 0.0), axis=1, keepdims=True)
        return jnp.broadcast_to(column * 0.5, (levels, cols))

    hp = per_level(push_v)
    hf = per_level(fill_v)
    vert = vert_v[...]
    vert_hi = vert.astype(jnp.bfloat16).astype(jnp.float32)
    vert_cat = jnp.concatenate([vert_hi, vert_hi, vert - vert_hi], axis=1).astype(
        jnp.bfloat16
    )
    mask = jnp.where(comp == 1, land_v[...].astype(jnp.float32), 1.0)

    def level_rows(y):
        return pl.ds(y, levels, stride=rows)

    def back(x):
        return jnp.where(first, 0.0, pltpu.roll(x, 1, 1))

    def ahead(x):
        return jnp.where(last, 0.0, pltpu.roll(x, cols - 1, 1))

    spread = jnp.broadcast_to
    groups = levels // 8
    lane8 = lane[:8]
    side_angle = ((lane8 // 4 + lat * rows).astype(jnp.float32) + 0.5) / (n_lat * rows) - 0.5
    side_fcor = CORIOLIS * jnp.sin(math.pi * side_angle)
    side_fcor = jnp.concatenate([side_fcor] * groups, axis=0)
    owner = lane // 4

    def gather(take):
        first_row = take(0)
        result = jnp.zeros_like(first_row)
        for y in range(rows):
            value = first_row if y == 0 else take(y)
            turned = pltpu.roll(value, 4 * y + 2, 1)
            result = jnp.where(owner[: value.shape[0]] == y, turned, result)
        return result

    side_mask = gather(lambda y: spread(mask[y : y + 1], (8, cols)))
    side_mask = jnp.concatenate([side_mask] * groups, axis=0)

    def split(x):
        hi = x.astype(jnp.bfloat16)
        lo = (x - hi.astype(jnp.float32)).astype(jnp.bfloat16)
        return jnp.concatenate([hi, lo, hi], axis=0)

    def remote(src, dst, k, to):
        return pltpu.make_async_remote_copy(
            src_ref=src,
            dst_ref=dst,
            send_sem=send_sem.at[k],
            recv_sem=recv_sem.at[k],
            device_id=to,
            device_id_type=MESH,
        )

    sends = []
    surf_sends = []

    def send_sides(step, p_side, u_side, v_side):
        inner = jnp.where(quad == 1, pltpu.roll(p_side, 1, 1), -pltpu.roll(p_side, cols - 1, 1))
        w_side = u_side + side_fcor * v_side + hp * inner
        packed = jnp.where(lane < 4 * rows, p_side, pltpu.roll(w_side, 4 * rows, 1))
        for k in (0, 1):
            dense = jnp.zeros((8, cols), jnp.float32)
            for g in range(groups):
                turn = (g - 1 - k) % cols
                part = packed[8 * g : 8 * g + 8]
                part = pltpu.roll(part, turn, 1) if turn else part
                dense = jnp.where(quad[:8] == g, part, dense)
            pack[step, k] = dense
        if step == 0:
            pl.semaphore_wait(barrier, 7)
        base = 3 + 4 * step
        lo = remote(pack.at[step, 0], from_lo.at[step], base, (comp, lat, east))
        hi = remote(pack.at[step, 1], from_hi.at[step], base + 1, (comp, lat, west))
        for copy in (hi, lo):
            copy.start()
            sends.append(copy)
        return packed, lo, hi

    def raw_row(f, y):
        return raw[pl.ds(f * plane + y, levels, stride=rows), :]

    def first_p(y):
        p = raw_row(2, y)
        pres[y] = p
        return p

    side = send_sides(
        0,
        gather(first_p),
        gather(functools.partial(raw_row, 0)),
        gather(functools.partial(raw_row, 1)),
    )
    for step in range(STEPS):
        base = 3 + 4 * step
        packed, lo, hi = side

        def get(f, y):
            return raw_row(f, y) if step == 0 else (unew, vnew, pres)[f][y]

        for y in (0, rows - 1):
            v1 = get(1, y) - fcor[y : y + 1] * get(0, y)
            v1 = v1 - hp * pres[y + 1] if y == 0 else v1 + hp * pres[y - 1]
            vone[y] = v1
            k = 0 if y == 0 else 1
            edge[step, k, 0] = pres[y]
            edge[step, k, 1] = v1
        down = remote(edge.at[step, 0], row_hi.at[step], base + 2, (comp, south, lon))
        up = remote(edge.at[step, 1], row_lo.at[step], base + 3, (comp, north, lon))
        for copy in (down, up):
            copy.start()
            sends.append(copy)
        if step == 0:
            for k, to in enumerate((lon, east, west)):
                for f in range(3):
                    copy = remote(
                        raw.at[pl.ds(f * plane, rows)],
                        surf.at[k, f],
                        3 + 4 * STEPS + 3 * k + f,
                        (other, lat, to),
                    )
                    copy.start()
                    surf_sends.append(copy)

        for y in range(1, rows - 1):
            vone[y] = (
                get(1, y) - fcor[y : y + 1] * get(0, y) - hp * (pres[y + 1] - pres[y - 1])
            )
        for y in range(rows):
            p = pres[y]
            uone[y] = get(0, y) + fcor[y : y + 1] * get(1, y) - hp * (ahead(p) - back(p))
        for y in range(rows):
            u1 = uone[y]
            div = ahead(u1) - back(u1)
            if y + 1 < rows:
                div = div + vone[y + 1]
            if y > 0:
                div = div - vone[y - 1]
            pone[y] = pres[y] - hf * div

        down.wait_recv()
        up.wait_recv()
        p_lo = has_south * row_lo[step, 0]
        p_hi = has_north * row_hi[step, 0]
        v_lo = has_south * (row_lo[step, 1] - hp * pres[0])
        v_hi = has_north * (row_hi[step, 1] + hp * pres[rows - 1])
        fix_lo = hp * p_lo
        fix_hi = -hp * p_hi
        vone[0] = vone[0] + fix_lo
        vone[rows - 1] = vone[rows - 1] + fix_hi
        pone[0] = pone[0] + hf * v_lo
        pone[1] = pone[1] + hf * fix_lo
        pone[rows - 1] = pone[rows - 1] - hf * v_hi
        pone[rows - 2] = pone[rows - 2] - hf * fix_hi

        if step + 1 < STEPS:
            p_side = gather(lambda y: pone[y])
            u_edge = gather(lambda y: uone[y])
            v_edge = gather(lambda y: vone[y])
        lo.wait_recv()
        hi.wait_recv()
        moved = []
        for g in range(groups):
            low, high = (
                pltpu.roll(box[step], turn % cols, 1) if turn else box[step]
                for box, turn in ((from_lo, 2 - g), (from_hi, 1 - g))
            )
            moved.append(jnp.where(quad[:8] == 1, high, low))
        moved = jnp.concatenate(moved, axis=0)
        signed = jnp.where(quad == 1, hp, -hp)
        u_side = pltpu.roll(moved, cols - 4 * rows, 1) + signed * packed
        u_fix = -signed * moved
        d_fix = jnp.where(
            quad == 1,
            u_side,
            jnp.where(
                quad == 2,
                -u_side,
                jnp.where(
                    quad == 0, pltpu.roll(u_fix, cols - 1, 1), -pltpu.roll(u_fix, 1, 1)
                ),
            ),
        )
        d_fix = hf * d_fix
        ends = first | last
        near = (lane < 2) | (lane > cols - 3)
        if step + 1 < STEPS:
            p_side = jnp.dot(
                vert_cat, split(p_side - d_fix), preferred_element_type=jnp.float32
            )
            side = send_sides(
                step + 1,
                side_mask * p_side,
                side_mask * (u_edge + u_fix),
                side_mask * v_edge,
            )
        pieces = []
        for y in range(rows):
            turn = cols - (4 * y + 2)
            uone[y] = uone[y] + jnp.where(ends, pltpu.roll(u_fix, turn, 1), 0.0)
            p1 = pone[y] - jnp.where(near, pltpu.roll(d_fix, turn, 1), 0.0)
            pieces.append(split(p1))
        p2 = jnp.dot(
            vert_cat, jnp.concatenate(pieces, axis=1), preferred_element_type=jnp.float32
        )
        for y in range(rows):
            keep = mask[y : y + 1]
            u2 = keep * uone[y]
            v2 = keep * vone[y]
            pn = keep * p2[:, y * cols : (y + 1) * cols]
            if step + 1 < STEPS:
                unew[y] = u2
                vnew[y] = v2
                pres[y] = pn
            else:
                for f, value in enumerate((u2, v2, pn)):
                    out[pl.ds(f * plane + y, levels, stride=rows), :] = value

    count = count_v[...].astype(jnp.float32)
    match = match_v[...]
    tile = lax.broadcasted_iota(jnp.int32, match.shape, 1)

    def coef(peer):
        own = jnp.where((tile == lon) & (match == peer), count, 0.0)
        theirs = jnp.where((tile == peer) & (match == lon), count, 0.0)
        picked = jnp.where(comp == 1, own, theirs)
        total = jnp.sum(jnp.sum(picked, axis=1, keepdims=True), axis=0, keepdims=True)
        return jnp.broadcast_to(total, (rows, cols))

    coefs = [coef(lon), coef(west), coef(east)]
    inverse = KAPPA * mask / (coefs[0] + coefs[1] + coefs[2])
    scaled = [c * inverse for c in coefs]
    for copy in surf_sends:
        copy.wait_recv()
    for f in range(3):
        at = pl.ds(f * plane, rows)
        flux = -KAPPA * mask * raw[at]
        for k in range(3):
            flux = flux + scaled[k] * surf[k, f]
        out[at] = out[at] + flux
    for copy in sends + surf_sends:
        copy.wait_send()


def shards(n_lat, n_lon, state, push, fill, vertical, land, match, counts):
    _, fields, levels, rows, cols = state.shape
    assert fields == 3 and 8 * rows <= cols and levels % 8 == 0 and levels <= 32
    block = (rows, levels, cols)
    n_sems = 3 + 4 * STEPS + 9
    f32 = jnp.float32
    any_spec = pl.BlockSpec(memory_space=pl.ANY)
    result = pl.pallas_call(
        functools.partial(kernel, (levels, rows, cols, n_lat, n_lon)),
        out_shape=pltpu.VMEM((fields * levels * rows, cols), f32),
        in_specs=[any_spec] * 7,
        out_specs=pl.BlockSpec(memory_space=pltpu.VMEM),
        scratch_shapes=[
            pltpu.VMEM((fields * levels * rows, cols), f32),
            pltpu.VMEM(push.shape, f32),
            pltpu.VMEM(fill.shape, f32),
            pltpu.VMEM(vertical.shape[1:], f32),
            pltpu.VMEM(land.shape, jnp.int32),
            pltpu.VMEM(match.shape[:0:-1], jnp.int32),
            pltpu.VMEM(counts.shape[:0:-1], jnp.int32),
            pltpu.VMEM(block, f32),
            pltpu.VMEM(block, f32),
            pltpu.VMEM(block, f32),
            pltpu.VMEM(block, f32),
            pltpu.VMEM(block, f32),
            pltpu.VMEM(block, f32),
            pltpu.VMEM((STEPS, 2, 8, cols), f32),
            pltpu.VMEM((STEPS, 8, cols), f32),
            pltpu.VMEM((STEPS, 8, cols), f32),
            pltpu.VMEM((STEPS, 2, 2, levels, cols), f32),
            pltpu.VMEM((STEPS, 2, levels, cols), f32),
            pltpu.VMEM((STEPS, 2, levels, cols), f32),
            pltpu.VMEM((3, fields, rows, cols), f32),
            pltpu.SemaphoreType.DMA((9,)),
            pltpu.SemaphoreType.DMA((n_sems,)),
            pltpu.SemaphoreType.DMA((n_sems,)),
        ],
        compiler_params=pltpu.CompilerParams(collective_id=0, has_side_effects=True),
        name="window",
    )(
        state.reshape(fields * levels * rows, cols),
        push,
        fill,
        vertical.reshape(vertical.shape[1:]),
        land,
        match[0].T,
        counts[0].T,
    )
    return result.reshape(state.shape)


def solution(mesh):
    sizes = dict(mesh.shape)
    return jax.shard_map(
        functools.partial(shards, sizes["lat"], sizes["lon"]),
        mesh=mesh,
        in_specs=(
            P("comp", None, None, "lat", "lon"),
            P("comp", None),
            P("comp", None),
            P("comp", None, None),
            P("lat", "lon"),
            P("lat", None, None),
            P("lat", None, None),
        ),
        out_specs=P("comp", None, None, "lat", "lon"),
        check_vma=False,
    )
```

```python
import functools
import math

import jax
import jax.numpy as jnp
from jax import lax
from jax.experimental import pallas as pl
from jax.experimental.pallas import tpu as pltpu
from jax.sharding import PartitionSpec as P

KAPPA = 0.5
CORIOLIS = 0.4
MESH = pl.DeviceIdType.MESH
STEPS = 2


def kernel(
    sizes,
    state,
    push_in,
    fill_in,
    vert_in,
    land_in,
    match_in,
    count_in,
    out,
    raw,
    push_v,
    fill_v,
    vert_v,
    land_v,
    match_v,
    count_v,
    pres,
    uone,
    vone,
    pone,
    unew,
    vnew,
    pack,
    from_lo,
    from_hi,
    edge,
    row_lo,
    row_hi,
    surf,
    load_sem,
    send_sem,
    recv_sem,
):
    levels, rows, cols, n_lat, n_lon = sizes
    comp = lax.axis_index("comp")
    lat = lax.axis_index("lat")
    lon = lax.axis_index("lon")
    west = lax.rem(lon + n_lon - 1, n_lon)
    east = lax.rem(lon + 1, n_lon)
    south = lax.rem(lat + n_lat - 1, n_lat)
    north = lax.rem(lat + 1, n_lat)
    other = 1 - comp
    plane = levels * rows

    barrier = pltpu.get_barrier_semaphore()
    for to in (
        (comp, lat, west),
        (comp, lat, east),
        (comp, south, lon),
        (comp, north, lon),
        (other, lat, lon),
        (other, lat, west),
        (other, lat, east),
    ):
        pl.semaphore_signal(barrier, inc=1, device_id=to, device_id_type=MESH)

    loads = []
    for f in (2, 0, 1):
        loads.append(
            pltpu.make_async_copy(
                state.at[pl.ds(f * plane, plane)],
                raw.at[pl.ds(f * plane, plane)],
                load_sem.at[f],
            )
        )
    for k, (src, dst) in enumerate(
        (
            (push_in, push_v),
            (fill_in, fill_v),
            (vert_in, vert_v),
            (land_in, land_v),
            (match_in, match_v),
            (count_in, count_v),
        )
    ):
        loads.append(pltpu.make_async_copy(src, dst, load_sem.at[3 + k]))
    for copy in loads:
        copy.start()

    lane = lax.broadcasted_iota(jnp.int32, (levels, cols), 1)
    first = lane == 0
    last = lane == cols - 1
    quad = lax.rem(lane, 4)
    row_id = lax.broadcasted_iota(jnp.int32, (rows, cols), 0) + lat * rows
    angle = (row_id.astype(jnp.float32) + 0.5) / (n_lat * rows) - 0.5
    fcor = CORIOLIS * jnp.sin(math.pi * angle)
    has_south = (lat > 0).astype(jnp.float32)
    has_north = (lat < n_lat - 1).astype(jnp.float32)

    for copy in loads:
        copy.wait()

    diag = lax.broadcasted_iota(jnp.int32, (levels, levels), 0) == lax.broadcasted_iota(
        jnp.int32, (levels, levels), 1
    )

    def per_level(ref):
        wide = jnp.broadcast_to(ref[...], (levels, levels))
        column = jnp.sum(jnp.where(diag, wide, 0.0), axis=1, keepdims=True)
        return jnp.broadcast_to(column * 0.5, (levels, cols))

    hp = per_level(push_v)
    hf = per_level(fill_v)
    vert = vert_v[...]
    vert_hi = vert.astype(jnp.bfloat16).astype(jnp.float32)
    vert_cat = jnp.concatenate([vert_hi, vert_hi, vert - vert_hi], axis=1).astype(
        jnp.bfloat16
    )
    mask = jnp.where(comp == 1, land_v[...].astype(jnp.float32), 1.0)

    def level_rows(y):
        return pl.ds(y, levels, stride=rows)

    def back(x):
        return jnp.where(first, 0.0, pltpu.roll(x, 1, 1))

    def ahead(x):
        return jnp.where(last, 0.0, pltpu.roll(x, cols - 1, 1))

    spread = jnp.broadcast_to
    groups = levels // 8
    lane8 = lane[:8]
    side_angle = ((lane8 // 4 + lat * rows).astype(jnp.float32) + 0.5) / (n_lat * rows) - 0.5
    side_fcor = CORIOLIS * jnp.sin(math.pi * side_angle)
    side_fcor = jnp.concatenate([side_fcor] * groups, axis=0)
    owner = lane // 4

    def gather(take):
        first_row = take(0)
        result = jnp.zeros_like(first_row)
        for y in range(rows):
            value = first_row if y == 0 else take(y)
            turned = pltpu.roll(value, 4 * y + 2, 1)
            result = jnp.where(owner[: value.shape[0]] == y, turned, result)
        return result

    side_mask = gather(lambda y: spread(mask[y : y + 1], (8, cols)))
    side_mask = jnp.concatenate([side_mask] * groups, axis=0)

    def split(x):
        hi = x.astype(jnp.bfloat16)
        lo = (x - hi.astype(jnp.float32)).astype(jnp.bfloat16)
        return jnp.concatenate([hi, lo, hi], axis=0)

    def remote(src, dst, k, to):
        return pltpu.make_async_remote_copy(
            src_ref=src,
            dst_ref=dst,
            send_sem=send_sem.at[k],
            recv_sem=recv_sem.at[k],
            device_id=to,
            device_id_type=MESH,
        )

    sends = []
    surf_sends = []

    def send_sides(step, p_side, u_side, v_side):
        inner = jnp.where(quad == 1, pltpu.roll(p_side, 1, 1), -pltpu.roll(p_side, cols - 1, 1))
        w_side = u_side + side_fcor * v_side + hp * inner
        packed = jnp.where(lane < 4 * rows, p_side, pltpu.roll(w_side, 4 * rows, 1))
        for k in (0, 1):
            dense = jnp.zeros((8, cols), jnp.float32)
            for g in range(groups):
                turn = (g - 1 - k) % cols
                part = packed[8 * g : 8 * g + 8]
                part = pltpu.roll(part, turn, 1) if turn else part
                dense = jnp.where(quad[:8] == g, part, dense)
            pack[step, k] = dense
        if step == 0:
            pl.semaphore_wait(barrier, 7)
        base = 3 + 4 * step
        lo = remote(pack.at[step, 0], from_lo.at[step], base, (comp, lat, east))
        hi = remote(pack.at[step, 1], from_hi.at[step], base + 1, (comp, lat, west))
        for copy in (hi, lo):
            copy.start()
            sends.append(copy)
        return packed, lo, hi

    def raw_row(f, y):
        return raw[pl.ds(f * plane + y, levels, stride=rows), :]

    def first_p(y):
        p = raw_row(2, y)
        pres[y] = p
        return p

    side = send_sides(
        0,
        gather(first_p),
        gather(functools.partial(raw_row, 0)),
        gather(functools.partial(raw_row, 1)),
    )
    def add_flux():
        count = count_v[...].astype(jnp.float32)
        match = match_v[...]
        tile = lax.broadcasted_iota(jnp.int32, match.shape, 1)

        def coef(peer):
            own = jnp.where((tile == lon) & (match == peer), count, 0.0)
            theirs = jnp.where((tile == peer) & (match == lon), count, 0.0)
            picked = jnp.where(comp == 1, own, theirs)
            total = jnp.sum(jnp.sum(picked, axis=1, keepdims=True), axis=0, keepdims=True)
            return jnp.broadcast_to(total, (rows, cols))

        coefs = [coef(lon), coef(west), coef(east)]
        inverse = KAPPA * mask / (coefs[0] + coefs[1] + coefs[2])
        scaled = [c * inverse for c in coefs]
        for copy in surf_sends:
            copy.wait_recv()
        for f in range(3):
            at = pl.ds(f * plane, rows)
            flux = -KAPPA * mask * raw[at]
            for k in range(3):
                flux = flux + scaled[k] * surf[k, f]
            out[at] = out[at] + flux

    for step in range(STEPS):
        base = 3 + 4 * step
        packed, lo, hi = side

        def get(f, y):
            return raw_row(f, y) if step == 0 else (unew, vnew, pres)[f][y]

        for y in (0, rows - 1):
            v1 = get(1, y) - fcor[y : y + 1] * get(0, y)
            v1 = v1 - hp * pres[y + 1] if y == 0 else v1 + hp * pres[y - 1]
            vone[y] = v1
            k = 0 if y == 0 else 1
            edge[step, k, 0] = pres[y]
            edge[step, k, 1] = v1
        down = remote(edge.at[step, 0], row_hi.at[step], base + 2, (comp, south, lon))
        up = remote(edge.at[step, 1], row_lo.at[step], base + 3, (comp, north, lon))
        for copy in (down, up):
            copy.start()
            sends.append(copy)
        if step == 0:
            for k, to in enumerate((lon, east, west)):
                for f in range(3):
                    copy = remote(
                        raw.at[pl.ds(f * plane, rows)],
                        surf.at[k, f],
                        3 + 4 * STEPS + 3 * k + f,
                        (other, lat, to),
                    )
                    copy.start()
                    surf_sends.append(copy)

        for y in range(1, rows - 1):
            vone[y] = (
                get(1, y) - fcor[y : y + 1] * get(0, y) - hp * (pres[y + 1] - pres[y - 1])
            )
        for y in range(rows):
            p = pres[y]
            uone[y] = get(0, y) + fcor[y : y + 1] * get(1, y) - hp * (ahead(p) - back(p))
        for y in range(rows):
            u1 = uone[y]
            div = ahead(u1) - back(u1)
            if y + 1 < rows:
                div = div + vone[y + 1]
            if y > 0:
                div = div - vone[y - 1]
            pone[y] = pres[y] - hf * div

        down.wait_recv()
        up.wait_recv()
        p_lo = has_south * row_lo[step, 0]
        p_hi = has_north * row_hi[step, 0]
        v_lo = has_south * (row_lo[step, 1] - hp * pres[0])
        v_hi = has_north * (row_hi[step, 1] + hp * pres[rows - 1])
        fix_lo = hp * p_lo
        fix_hi = -hp * p_hi
        vone[0] = vone[0] + fix_lo
        vone[rows - 1] = vone[rows - 1] + fix_hi
        pone[0] = pone[0] + hf * v_lo
        pone[1] = pone[1] + hf * fix_lo
        pone[rows - 1] = pone[rows - 1] - hf * v_hi
        pone[rows - 2] = pone[rows - 2] - hf * fix_hi

        if step + 1 < STEPS:
            p_side = gather(lambda y: pone[y])
            u_edge = gather(lambda y: uone[y])
            v_edge = gather(lambda y: vone[y])
        else:
            p2 = jnp.dot(
                vert_cat,
                jnp.concatenate([split(pone[y]) for y in range(rows)], axis=1),
                preferred_element_type=jnp.float32,
            )
            for y in range(rows):
                keep = mask[y : y + 1]
                pn = p2[:, y * cols : (y + 1) * cols]
                for f, value in enumerate((uone[y], vone[y], pn)):
                    out[pl.ds(f * plane + y, levels, stride=rows), :] = keep * value
            add_flux()
        lo.wait_recv()
        hi.wait_recv()
        moved = []
        for g in range(groups):
            low, high = (
                pltpu.roll(box[step], turn % cols, 1) if turn else box[step]
                for box, turn in ((from_lo, 2 - g), (from_hi, 1 - g))
            )
            moved.append(jnp.where(quad[:8] == 1, high, low))
        moved = jnp.concatenate(moved, axis=0)
        signed = jnp.where(quad == 1, hp, -hp)
        u_side = pltpu.roll(moved, cols - 4 * rows, 1) + signed * packed
        u_fix = -signed * moved
        d_fix = jnp.where(
            quad == 1,
            u_side,
            jnp.where(
                quad == 2,
                -u_side,
                jnp.where(
                    quad == 0, pltpu.roll(u_fix, cols - 1, 1), -pltpu.roll(u_fix, 1, 1)
                ),
            ),
        )
        d_fix = hf * d_fix
        ends = first | last
        near = (lane < 2) | (lane > cols - 3)
        if step + 1 == STEPS:
            p_fix = -side_mask * jnp.dot(
                vert_cat, split(d_fix), preferred_element_type=jnp.float32
            )
            u_fix = side_mask * u_fix
            for y in range(rows):
                turn = cols - (4 * y + 2)
                for f, fix, where in ((0, u_fix, ends), (2, p_fix, near)):
                    at = pl.ds(f * plane + y, levels, stride=rows)
                    out[at, :] = out[at, :] + jnp.where(where, pltpu.roll(fix, turn, 1), 0.0)
            break
        p_side = jnp.dot(vert_cat, split(p_side - d_fix), preferred_element_type=jnp.float32)
        side = send_sides(
            step + 1,
            side_mask * p_side,
            side_mask * (u_edge + u_fix),
            side_mask * v_edge,
        )
        pieces = []
        for y in range(rows):
            turn = cols - (4 * y + 2)
            uone[y] = uone[y] + jnp.where(ends, pltpu.roll(u_fix, turn, 1), 0.0)
            p1 = pone[y] - jnp.where(near, pltpu.roll(d_fix, turn, 1), 0.0)
            pieces.append(split(p1))
        p2 = jnp.dot(
            vert_cat, jnp.concatenate(pieces, axis=1), preferred_element_type=jnp.float32
        )
        for y in range(rows):
            keep = mask[y : y + 1]
            unew[y] = keep * uone[y]
            vnew[y] = keep * vone[y]
            pres[y] = keep * p2[:, y * cols : (y + 1) * cols]

    for copy in sends + surf_sends:
        copy.wait_send()


def shards(n_lat, n_lon, state, push, fill, vertical, land, match, counts):
    _, fields, levels, rows, cols = state.shape
    assert fields == 3 and 8 * rows <= cols and levels % 8 == 0 and levels <= 32
    block = (rows, levels, cols)
    n_sems = 3 + 4 * STEPS + 9
    f32 = jnp.float32
    any_spec = pl.BlockSpec(memory_space=pl.ANY)
    result = pl.pallas_call(
        functools.partial(kernel, (levels, rows, cols, n_lat, n_lon)),
        out_shape=pltpu.VMEM((fields * levels * rows, cols), f32),
        in_specs=[any_spec] * 7,
        out_specs=pl.BlockSpec(memory_space=pltpu.VMEM),
        scratch_shapes=[
            pltpu.VMEM((fields * levels * rows, cols), f32),
            pltpu.VMEM(push.shape, f32),
            pltpu.VMEM(fill.shape, f32),
            pltpu.VMEM(vertical.shape[1:], f32),
            pltpu.VMEM(land.shape, jnp.int32),
            pltpu.VMEM(match.shape[:0:-1], jnp.int32),
            pltpu.VMEM(counts.shape[:0:-1], jnp.int32),
            pltpu.VMEM(block, f32),
            pltpu.VMEM(block, f32),
            pltpu.VMEM(block, f32),
            pltpu.VMEM(block, f32),
            pltpu.VMEM(block, f32),
            pltpu.VMEM(block, f32),
            pltpu.VMEM((STEPS, 2, 8, cols), f32),
            pltpu.VMEM((STEPS, 8, cols), f32),
            pltpu.VMEM((STEPS, 8, cols), f32),
            pltpu.VMEM((STEPS, 2, 2, levels, cols), f32),
            pltpu.VMEM((STEPS, 2, levels, cols), f32),
            pltpu.VMEM((STEPS, 2, levels, cols), f32),
            pltpu.VMEM((3, fields, rows, cols), f32),
            pltpu.SemaphoreType.DMA((9,)),
            pltpu.SemaphoreType.DMA((n_sems,)),
            pltpu.SemaphoreType.DMA((n_sems,)),
        ],
        compiler_params=pltpu.CompilerParams(collective_id=0, has_side_effects=True),
        name="window",
    )(
        state.reshape(fields * levels * rows, cols),
        push,
        fill,
        vertical.reshape(vertical.shape[1:]),
        land,
        match[0].T,
        counts[0].T,
    )
    return result.reshape(state.shape)


def solution(mesh):
    sizes = dict(mesh.shape)
    return jax.shard_map(
        functools.partial(shards, sizes["lat"], sizes["lon"]),
        mesh=mesh,
        in_specs=(
            P("comp", None, None, "lat", "lon"),
            P("comp", None),
            P("comp", None),
            P("comp", None, None),
            P("lat", "lon"),
            P("lat", None, None),
            P("lat", None, None),
        ),
        out_specs=P("comp", None, None, "lat", "lon"),
        check_vma=False,
    )
```

```python
import functools
import math

import jax
import jax.numpy as jnp
from jax import lax
from jax.experimental import pallas as pl
from jax.experimental.pallas import tpu as pltpu
from jax.sharding import PartitionSpec as P

KAPPA = 0.5
CORIOLIS = 0.4
MESH = pl.DeviceIdType.MESH
STEPS = 2


def kernel(
    sizes,
    state,
    push_in,
    fill_in,
    vert_in,
    land_in,
    match_in,
    count_in,
    out,
    raw,
    push_v,
    fill_v,
    vert_v,
    land_v,
    match_v,
    count_v,
    pres,
    uone,
    vone,
    pone,
    unew,
    vnew,
    pack,
    from_lo,
    from_hi,
    edge,
    row_lo,
    row_hi,
    surf,
    load_sem,
    send_sem,
    recv_sem,
):
    levels, rows, cols, n_lat, n_lon = sizes
    comp = lax.axis_index("comp")
    lat = lax.axis_index("lat")
    lon = lax.axis_index("lon")
    west = lax.rem(lon + n_lon - 1, n_lon)
    east = lax.rem(lon + 1, n_lon)
    south = lax.rem(lat + n_lat - 1, n_lat)
    north = lax.rem(lat + 1, n_lat)
    other = 1 - comp
    plane = levels * rows

    barrier = pltpu.get_barrier_semaphore()
    for to in (
        (comp, lat, west),
        (comp, lat, east),
        (comp, south, lon),
        (comp, north, lon),
        (other, lat, lon),
    ):
        pl.semaphore_signal(barrier, inc=1, device_id=to, device_id_type=MESH)

    loads = []
    for f in (2, 0, 1):
        loads.append(
            pltpu.make_async_copy(
                state.at[pl.ds(f * plane, plane)],
                raw.at[pl.ds(f * plane, plane)],
                load_sem.at[f],
            )
        )
    for k, (src, dst) in enumerate(
        (
            (push_in, push_v),
            (fill_in, fill_v),
            (vert_in, vert_v),
            (land_in, land_v),
            (match_in, match_v),
            (count_in, count_v),
        )
    ):
        loads.append(pltpu.make_async_copy(src, dst, load_sem.at[3 + k]))
    for copy in loads:
        copy.start()

    lane = lax.broadcasted_iota(jnp.int32, (levels, cols), 1)
    first = lane == 0
    last = lane == cols - 1
    quad = lax.rem(lane, 4)
    row_id = lax.broadcasted_iota(jnp.int32, (rows, cols), 0) + lat * rows
    angle = (row_id.astype(jnp.float32) + 0.5) / (n_lat * rows) - 0.5
    fcor = CORIOLIS * jnp.sin(math.pi * angle)
    has_south = (lat > 0).astype(jnp.float32)
    has_north = (lat < n_lat - 1).astype(jnp.float32)

    for copy in loads:
        copy.wait()

    diag = lax.broadcasted_iota(jnp.int32, (levels, levels), 0) == lax.broadcasted_iota(
        jnp.int32, (levels, levels), 1
    )

    def per_level(ref):
        wide = jnp.broadcast_to(ref[...], (levels, levels))
        column = jnp.sum(jnp.where(diag, wide, 0.0), axis=1, keepdims=True)
        return jnp.broadcast_to(column * 0.5, (levels, cols))

    hp = per_level(push_v)
    hf = per_level(fill_v)
    vert = vert_v[...]
    vert_hi = vert.astype(jnp.bfloat16).astype(jnp.float32)
    vert_cat = jnp.concatenate([vert_hi, vert_hi, vert - vert_hi], axis=1).astype(
        jnp.bfloat16
    )
    mask = jnp.where(comp == 1, land_v[...].astype(jnp.float32), 1.0)

    def level_rows(y):
        return pl.ds(y, levels, stride=rows)

    def back(x):
        return jnp.where(first, 0.0, pltpu.roll(x, 1, 1))

    def ahead(x):
        return jnp.where(last, 0.0, pltpu.roll(x, cols - 1, 1))

    spread = jnp.broadcast_to
    groups = levels // 8
    lane8 = lane[:8]
    side_angle = ((lane8 // 4 + lat * rows).astype(jnp.float32) + 0.5) / (n_lat * rows) - 0.5
    side_fcor = CORIOLIS * jnp.sin(math.pi * side_angle)
    side_fcor = jnp.concatenate([side_fcor] * groups, axis=0)
    owner = lane // 4

    def gather(take):
        first_row = take(0)
        result = jnp.zeros_like(first_row)
        for y in range(rows):
            value = first_row if y == 0 else take(y)
            turned = pltpu.roll(value, 4 * y + 2, 1)
            result = jnp.where(owner[: value.shape[0]] == y, turned, result)
        return result

    side_mask = gather(lambda y: spread(mask[y : y + 1], (8, cols)))
    side_mask = jnp.concatenate([side_mask] * groups, axis=0)

    def split(x):
        hi = x.astype(jnp.bfloat16)
        lo = (x - hi.astype(jnp.float32)).astype(jnp.bfloat16)
        return jnp.concatenate([hi, lo, hi], axis=0)

    def remote(src, dst, k, to):
        return pltpu.make_async_remote_copy(
            src_ref=src,
            dst_ref=dst,
            send_sem=send_sem.at[k],
            recv_sem=recv_sem.at[k],
            device_id=to,
            device_id_type=MESH,
        )

    sends = []
    surf_sends = []
    surf_first = []

    def send_sides(step, p_side, u_side, v_side):
        inner = jnp.where(quad == 1, pltpu.roll(p_side, 1, 1), -pltpu.roll(p_side, cols - 1, 1))
        w_side = u_side + side_fcor * v_side + hp * inner
        packed = jnp.where(lane < 4 * rows, p_side, pltpu.roll(w_side, 4 * rows, 1))
        for k in (0, 1):
            dense = jnp.zeros((8, cols), jnp.float32)
            for g in range(groups):
                turn = (g - 1 - k) % cols
                part = packed[8 * g : 8 * g + 8]
                part = pltpu.roll(part, turn, 1) if turn else part
                dense = jnp.where(quad[:8] == g, part, dense)
            pack[step, k] = dense
        if step == 0:
            pl.semaphore_wait(barrier, 5)
        base = 3 + 4 * step
        lo = remote(pack.at[step, 0], from_lo.at[step], base, (comp, lat, east))
        hi = remote(pack.at[step, 1], from_hi.at[step], base + 1, (comp, lat, west))
        for copy in (hi, lo):
            copy.start()
            sends.append(copy)
        return packed, lo, hi

    def raw_row(f, y):
        return raw[pl.ds(f * plane + y, levels, stride=rows), :]

    def first_p(y):
        p = raw_row(2, y)
        pres[y] = p
        return p

    side = send_sides(
        0,
        gather(first_p),
        gather(functools.partial(raw_row, 0)),
        gather(functools.partial(raw_row, 1)),
    )
    def add_flux():
        count = count_v[...].astype(jnp.float32)
        match = match_v[...]
        tile = lax.broadcasted_iota(jnp.int32, match.shape, 1)

        def coef(peer):
            own = jnp.where((tile == lon) & (match == peer), count, 0.0)
            theirs = jnp.where((tile == peer) & (match == lon), count, 0.0)
            picked = jnp.where(comp == 1, own, theirs)
            total = jnp.sum(jnp.sum(picked, axis=1, keepdims=True), axis=0, keepdims=True)
            return jnp.broadcast_to(total, (rows, cols))

        coefs = [coef(lon), coef(west), coef(east)]
        inverse = KAPPA * mask / (coefs[0] + coefs[1] + coefs[2])
        scaled = [c * inverse for c in coefs]
        for copy in surf_sends:
            copy.wait_recv()
        for f in range(3):
            at = pl.ds(f * plane, rows)
            flux = -KAPPA * mask * raw[at]
            for k in range(3):
                flux = flux + scaled[k] * surf[k, f]
            out[at] = out[at] + flux

    for step in range(STEPS):
        base = 3 + 4 * step
        packed, lo, hi = side

        def get(f, y):
            return raw_row(f, y) if step == 0 else (unew, vnew, pres)[f][y]

        for y in (0, rows - 1):
            v1 = get(1, y) - fcor[y : y + 1] * get(0, y)
            v1 = v1 - hp * pres[y + 1] if y == 0 else v1 + hp * pres[y - 1]
            vone[y] = v1
            k = 0 if y == 0 else 1
            edge[step, k, 0] = pres[y]
            edge[step, k, 1] = v1
        down = remote(edge.at[step, 0], row_hi.at[step], base + 2, (comp, south, lon))
        up = remote(edge.at[step, 1], row_lo.at[step], base + 3, (comp, north, lon))
        for copy in (down, up):
            copy.start()
            sends.append(copy)
        if step == 0:
            for f in range(3):
                copy = remote(
                    raw.at[pl.ds(f * plane, rows)],
                    surf.at[0, f],
                    3 + 4 * STEPS + f,
                    (other, lat, lon),
                )
                copy.start()
                sends.append(copy)
                surf_first.append(copy)

        for y in range(1, rows - 1):
            vone[y] = (
                get(1, y) - fcor[y : y + 1] * get(0, y) - hp * (pres[y + 1] - pres[y - 1])
            )
        for y in range(rows):
            p = pres[y]
            uone[y] = get(0, y) + fcor[y : y + 1] * get(1, y) - hp * (ahead(p) - back(p))
        for y in range(rows):
            u1 = uone[y]
            div = ahead(u1) - back(u1)
            if y + 1 < rows:
                div = div + vone[y + 1]
            if y > 0:
                div = div - vone[y - 1]
            pone[y] = pres[y] - hf * div

        down.wait_recv()
        up.wait_recv()
        p_lo = has_south * row_lo[step, 0]
        p_hi = has_north * row_hi[step, 0]
        v_lo = has_south * (row_lo[step, 1] - hp * pres[0])
        v_hi = has_north * (row_hi[step, 1] + hp * pres[rows - 1])
        fix_lo = hp * p_lo
        fix_hi = -hp * p_hi
        vone[0] = vone[0] + fix_lo
        vone[rows - 1] = vone[rows - 1] + fix_hi
        pone[0] = pone[0] + hf * v_lo
        pone[1] = pone[1] + hf * fix_lo
        pone[rows - 1] = pone[rows - 1] - hf * v_hi
        pone[rows - 2] = pone[rows - 2] - hf * fix_hi

        if step + 1 < STEPS:
            p_side = gather(lambda y: pone[y])
            u_edge = gather(lambda y: uone[y])
            v_edge = gather(lambda y: vone[y])
        else:
            p2 = jnp.dot(
                vert_cat,
                jnp.concatenate([split(pone[y]) for y in range(rows)], axis=1),
                preferred_element_type=jnp.float32,
            )
            for y in range(rows):
                keep = mask[y : y + 1]
                pn = p2[:, y * cols : (y + 1) * cols]
                for f, value in enumerate((uone[y], vone[y], pn)):
                    out[pl.ds(f * plane + y, levels, stride=rows), :] = keep * value
            add_flux()
        if step == 0:
            for copy in surf_first:
                copy.wait_recv()
            for k, to in ((1, east), (2, west)):
                copy = remote(surf.at[0], surf.at[k], 5 + 4 * STEPS + k, (comp, lat, to))
                copy.start()
                surf_sends.append(copy)
        lo.wait_recv()
        hi.wait_recv()
        moved = []
        for g in range(groups):
            low, high = (
                pltpu.roll(box[step], turn % cols, 1) if turn else box[step]
                for box, turn in ((from_lo, 2 - g), (from_hi, 1 - g))
            )
            moved.append(jnp.where(quad[:8] == 1, high, low))
        moved = jnp.concatenate(moved, axis=0)
        signed = jnp.where(quad == 1, hp, -hp)
        u_side = pltpu.roll(moved, cols - 4 * rows, 1) + signed * packed
        u_fix = -signed * moved
        d_fix = jnp.where(
            quad == 1,
            u_side,
            jnp.where(
                quad == 2,
                -u_side,
                jnp.where(
                    quad == 0, pltpu.roll(u_fix, cols - 1, 1), -pltpu.roll(u_fix, 1, 1)
                ),
            ),
        )
        d_fix = hf * d_fix
        ends = first | last
        near = (lane < 2) | (lane > cols - 3)
        if step + 1 == STEPS:
            p_fix = -side_mask * jnp.dot(
                vert_cat, split(d_fix), preferred_element_type=jnp.float32
            )
            u_fix = side_mask * u_fix
            for y in range(rows):
                turn = cols - (4 * y + 2)
                for f, fix, where in ((0, u_fix, ends), (2, p_fix, near)):
                    at = pl.ds(f * plane + y, levels, stride=rows)
                    out[at, :] = out[at, :] + jnp.where(where, pltpu.roll(fix, turn, 1), 0.0)
            break
        p_side = jnp.dot(vert_cat, split(p_side - d_fix), preferred_element_type=jnp.float32)
        side = send_sides(
            step + 1,
            side_mask * p_side,
            side_mask * (u_edge + u_fix),
            side_mask * v_edge,
        )
        pieces = []
        for y in range(rows):
            turn = cols - (4 * y + 2)
            uone[y] = uone[y] + jnp.where(ends, pltpu.roll(u_fix, turn, 1), 0.0)
            p1 = pone[y] - jnp.where(near, pltpu.roll(d_fix, turn, 1), 0.0)
            pieces.append(split(p1))
        p2 = jnp.dot(
            vert_cat, jnp.concatenate(pieces, axis=1), preferred_element_type=jnp.float32
        )
        for y in range(rows):
            keep = mask[y : y + 1]
            unew[y] = keep * uone[y]
            vnew[y] = keep * vone[y]
            pres[y] = keep * p2[:, y * cols : (y + 1) * cols]

    for copy in sends + surf_sends:
        copy.wait_send()


def shards(n_lat, n_lon, state, push, fill, vertical, land, match, counts):
    _, fields, levels, rows, cols = state.shape
    assert fields == 3 and 8 * rows <= cols and levels % 8 == 0 and levels <= 32
    block = (rows, levels, cols)
    n_sems = 3 + 4 * STEPS + 5
    f32 = jnp.float32
    any_spec = pl.BlockSpec(memory_space=pl.ANY)
    result = pl.pallas_call(
        functools.partial(kernel, (levels, rows, cols, n_lat, n_lon)),
        out_shape=pltpu.VMEM((fields * levels * rows, cols), f32),
        in_specs=[any_spec] * 7,
        out_specs=pl.BlockSpec(memory_space=pltpu.VMEM),
        scratch_shapes=[
            pltpu.VMEM((fields * levels * rows, cols), f32),
            pltpu.VMEM(push.shape, f32),
            pltpu.VMEM(fill.shape, f32),
            pltpu.VMEM(vertical.shape[1:], f32),
            pltpu.VMEM(land.shape, jnp.int32),
            pltpu.VMEM(match.shape[:0:-1], jnp.int32),
            pltpu.VMEM(counts.shape[:0:-1], jnp.int32),
            pltpu.VMEM(block, f32),
            pltpu.VMEM(block, f32),
            pltpu.VMEM(block, f32),
            pltpu.VMEM(block, f32),
            pltpu.VMEM(block, f32),
            pltpu.VMEM(block, f32),
            pltpu.VMEM((STEPS, 2, 8, cols), f32),
            pltpu.VMEM((STEPS, 8, cols), f32),
            pltpu.VMEM((STEPS, 8, cols), f32),
            pltpu.VMEM((STEPS, 2, 2, levels, cols), f32),
            pltpu.VMEM((STEPS, 2, levels, cols), f32),
            pltpu.VMEM((STEPS, 2, levels, cols), f32),
            pltpu.VMEM((3, fields, rows, cols), f32),
            pltpu.SemaphoreType.DMA((9,)),
            pltpu.SemaphoreType.DMA((n_sems,)),
            pltpu.SemaphoreType.DMA((n_sems,)),
        ],
        compiler_params=pltpu.CompilerParams(collective_id=0, has_side_effects=True),
        name="window",
    )(
        state.reshape(fields * levels * rows, cols),
        push,
        fill,
        vertical.reshape(vertical.shape[1:]),
        land,
        match[0].T,
        counts[0].T,
    )
    return result.reshape(state.shape)


def solution(mesh):
    sizes = dict(mesh.shape)
    return jax.shard_map(
        functools.partial(shards, sizes["lat"], sizes["lon"]),
        mesh=mesh,
        in_specs=(
            P("comp", None, None, "lat", "lon"),
            P("comp", None),
            P("comp", None),
            P("comp", None, None),
            P("lat", "lon"),
            P("lat", None, None),
            P("lat", None, None),
        ),
        out_specs=P("comp", None, None, "lat", "lon"),
        check_vma=False,
    )
```

```python
import functools
import math

import jax
import jax.numpy as jnp
from jax import lax
from jax.experimental import pallas as pl
from jax.experimental.pallas import tpu as pltpu
from jax.sharding import PartitionSpec as P

KAPPA = 0.5
CORIOLIS = 0.4
MESH = pl.DeviceIdType.MESH
STEPS = 2


def kernel(
    sizes,
    state,
    push_in,
    fill_in,
    vert_in,
    land_in,
    match_in,
    count_in,
    out,
    raw,
    push_v,
    fill_v,
    vert_v,
    land_v,
    match_v,
    count_v,
    pres,
    uone,
    vone,
    pone,
    unew,
    vnew,
    pack,
    from_lo,
    from_hi,
    edge,
    row_lo,
    row_hi,
    surf,
    load_sem,
    send_sem,
    recv_sem,
):
    levels, rows, cols, n_lat, n_lon = sizes
    comp = lax.axis_index("comp")
    lat = lax.axis_index("lat")
    lon = lax.axis_index("lon")
    west = lax.rem(lon + n_lon - 1, n_lon)
    east = lax.rem(lon + 1, n_lon)
    south = lax.rem(lat + n_lat - 1, n_lat)
    north = lax.rem(lat + 1, n_lat)
    other = 1 - comp
    plane = levels * rows

    barrier = pltpu.get_barrier_semaphore()
    for to in (
        (comp, lat, west),
        (comp, lat, east),
        (comp, south, lon),
        (comp, north, lon),
        (other, lat, lon),
    ):
        pl.semaphore_signal(barrier, inc=1, device_id=to, device_id_type=MESH)

    loads = []
    for f in (2, 0, 1):
        loads.append(
            pltpu.make_async_copy(
                state.at[pl.ds(f * plane, plane)],
                raw.at[pl.ds(f * plane, plane)],
                load_sem.at[f],
            )
        )
    for k, (src, dst) in enumerate(
        (
            (push_in, push_v),
            (fill_in, fill_v),
            (vert_in, vert_v),
            (land_in, land_v),
            (match_in, match_v),
            (count_in, count_v),
        )
    ):
        loads.append(pltpu.make_async_copy(src, dst, load_sem.at[3 + k]))
    for copy in loads:
        copy.start()

    lane = lax.broadcasted_iota(jnp.int32, (levels, cols), 1)
    first = lane == 0
    last = lane == cols - 1
    quad = lax.rem(lane, 4)
    row_id = lax.broadcasted_iota(jnp.int32, (rows, cols), 0) + lat * rows
    angle = (row_id.astype(jnp.float32) + 0.5) / (n_lat * rows) - 0.5
    fcor = CORIOLIS * jnp.sin(math.pi * angle)
    has_south = (lat > 0).astype(jnp.float32)
    has_north = (lat < n_lat - 1).astype(jnp.float32)

    for copy in loads:
        copy.wait()

    diag = lax.broadcasted_iota(jnp.int32, (levels, levels), 0) == lax.broadcasted_iota(
        jnp.int32, (levels, levels), 1
    )

    def per_level(ref):
        wide = jnp.broadcast_to(ref[...], (levels, levels))
        column = jnp.sum(jnp.where(diag, wide, 0.0), axis=1, keepdims=True)
        return jnp.broadcast_to(column * 0.5, (levels, cols))

    hp = per_level(push_v)
    hf = per_level(fill_v)
    vert = vert_v[...]
    vert_hi = vert.astype(jnp.bfloat16).astype(jnp.float32)
    vert_cat = jnp.concatenate([vert_hi, vert_hi, vert - vert_hi], axis=1).astype(
        jnp.bfloat16
    )
    mask = jnp.where(comp == 1, land_v[...].astype(jnp.float32), 1.0)

    def level_rows(y):
        return pl.ds(y, levels, stride=rows)

    def back(x):
        return jnp.where(first, 0.0, pltpu.roll(x, 1, 1))

    def ahead(x):
        return jnp.where(last, 0.0, pltpu.roll(x, cols - 1, 1))

    spread = jnp.broadcast_to
    groups = levels // 8
    lane8 = lane[:8]
    side_angle = ((lane8 // 4 + lat * rows).astype(jnp.float32) + 0.5) / (n_lat * rows) - 0.5
    side_fcor = CORIOLIS * jnp.sin(math.pi * side_angle)
    side_fcor = jnp.concatenate([side_fcor] * groups, axis=0)
    owner = lane // 4

    def gather(take):
        first_row = take(0)
        result = jnp.zeros_like(first_row)
        for y in range(rows):
            value = first_row if y == 0 else take(y)
            turned = pltpu.roll(value, 4 * y + 2, 1)
            result = jnp.where(owner[: value.shape[0]] == y, turned, result)
        return result

    side_mask = gather(lambda y: spread(mask[y : y + 1], (8, cols)))
    side_mask = jnp.concatenate([side_mask] * groups, axis=0)

    def split(x):
        hi = x.astype(jnp.bfloat16)
        lo = (x - hi.astype(jnp.float32)).astype(jnp.bfloat16)
        return jnp.concatenate([hi, lo, hi], axis=0)

    def remote(src, dst, k, to):
        return pltpu.make_async_remote_copy(
            src_ref=src,
            dst_ref=dst,
            send_sem=send_sem.at[k],
            recv_sem=recv_sem.at[k],
            device_id=to,
            device_id_type=MESH,
        )

    sends = []
    surf_sends = []
    surf_first = []

    def send_sides(step, p_side, u_side, v_side):
        inner = jnp.where(quad == 1, pltpu.roll(p_side, 1, 1), -pltpu.roll(p_side, cols - 1, 1))
        w_side = u_side + side_fcor * v_side + hp * inner
        for k in (0, 1):
            dense = jnp.zeros((8, cols), jnp.float32)
            for g in range(groups):
                turn = g - 1 - k
                p_part = p_side[8 * g : 8 * g + 8]
                p_part = pltpu.roll(p_part, turn % cols, 1) if turn else p_part
                w_part = pltpu.roll(w_side[8 * g : 8 * g + 8], 4 * rows + turn, 1)
                part = jnp.where(lane8 < 4 * rows, p_part, w_part)
                dense = jnp.where(quad[:8] == g, part, dense)
            pack[step, k] = dense
        if step == 0:
            pl.semaphore_wait(barrier, 5)
        base = 3 + 4 * step
        lo = remote(pack.at[step, 0], from_lo.at[step], base, (comp, lat, east))
        hi = remote(pack.at[step, 1], from_hi.at[step], base + 1, (comp, lat, west))
        for copy in (hi, lo):
            copy.start()
            sends.append(copy)
        return p_side, lo, hi

    def raw_row(f, y):
        return raw[pl.ds(f * plane + y, levels, stride=rows), :]

    def first_p(y):
        p = raw_row(2, y)
        pres[y] = p
        return p

    side = send_sides(
        0,
        gather(first_p),
        gather(functools.partial(raw_row, 0)),
        gather(functools.partial(raw_row, 1)),
    )
    def add_flux():
        count = count_v[...].astype(jnp.float32)
        match = match_v[...]
        tile = lax.broadcasted_iota(jnp.int32, match.shape, 1)

        def coef(peer):
            own = jnp.where((tile == lon) & (match == peer), count, 0.0)
            theirs = jnp.where((tile == peer) & (match == lon), count, 0.0)
            picked = jnp.where(comp == 1, own, theirs)
            total = jnp.sum(jnp.sum(picked, axis=1, keepdims=True), axis=0, keepdims=True)
            return jnp.broadcast_to(total, (rows, cols))

        coefs = [coef(lon), coef(west), coef(east)]
        inverse = KAPPA * mask / (coefs[0] + coefs[1] + coefs[2])
        scaled = [c * inverse for c in coefs]
        for copy in surf_sends:
            copy.wait_recv()
        for f in range(3):
            at = pl.ds(f * plane, rows)
            flux = -KAPPA * mask * raw[at]
            for k in range(3):
                flux = flux + scaled[k] * surf[k, f]
            out[at] = out[at] + flux

    for step in range(STEPS):
        base = 3 + 4 * step
        packed, lo, hi = side

        def get(f, y):
            return raw_row(f, y) if step == 0 else (unew, vnew, pres)[f][y]

        for y in (0, rows - 1):
            v1 = get(1, y) - fcor[y : y + 1] * get(0, y)
            v1 = v1 - hp * pres[y + 1] if y == 0 else v1 + hp * pres[y - 1]
            vone[y] = v1
            k = 0 if y == 0 else 1
            edge[step, k, 0] = pres[y]
            edge[step, k, 1] = v1
        down = remote(edge.at[step, 0], row_hi.at[step], base + 2, (comp, south, lon))
        up = remote(edge.at[step, 1], row_lo.at[step], base + 3, (comp, north, lon))
        for copy in (down, up):
            copy.start()
            sends.append(copy)
        if step == 0:
            for f in range(3):
                copy = remote(
                    raw.at[pl.ds(f * plane, rows)],
                    surf.at[0, f],
                    3 + 4 * STEPS + f,
                    (other, lat, lon),
                )
                copy.start()
                sends.append(copy)
                surf_first.append(copy)

        for y in range(1, rows - 1):
            vone[y] = (
                get(1, y) - fcor[y : y + 1] * get(0, y) - hp * (pres[y + 1] - pres[y - 1])
            )
        for y in range(rows):
            p = pres[y]
            uone[y] = get(0, y) + fcor[y : y + 1] * get(1, y) - hp * (ahead(p) - back(p))
        for y in range(rows):
            u1 = uone[y]
            div = ahead(u1) - back(u1)
            if y + 1 < rows:
                div = div + vone[y + 1]
            if y > 0:
                div = div - vone[y - 1]
            pone[y] = pres[y] - hf * div

        down.wait_recv()
        up.wait_recv()
        p_lo = has_south * row_lo[step, 0]
        p_hi = has_north * row_hi[step, 0]
        v_lo = has_south * (row_lo[step, 1] - hp * pres[0])
        v_hi = has_north * (row_hi[step, 1] + hp * pres[rows - 1])
        fix_lo = hp * p_lo
        fix_hi = -hp * p_hi
        vone[0] = vone[0] + fix_lo
        vone[rows - 1] = vone[rows - 1] + fix_hi
        pone[0] = pone[0] + hf * v_lo
        pone[1] = pone[1] + hf * fix_lo
        pone[rows - 1] = pone[rows - 1] - hf * v_hi
        pone[rows - 2] = pone[rows - 2] - hf * fix_hi

        if step + 1 < STEPS:
            p_side = gather(lambda y: pone[y])
            u_edge = gather(lambda y: uone[y])
            v_edge = gather(lambda y: vone[y])
        else:
            p2 = jnp.dot(
                vert_cat,
                jnp.concatenate([split(pone[y]) for y in range(rows)], axis=1),
                preferred_element_type=jnp.float32,
            )
            for y in range(rows):
                keep = mask[y : y + 1]
                pn = p2[:, y * cols : (y + 1) * cols]
                for f, value in enumerate((uone[y], vone[y], pn)):
                    out[pl.ds(f * plane + y, levels, stride=rows), :] = keep * value
            add_flux()
        if step == 0:
            for copy in surf_first:
                copy.wait_recv()
            for k, to in ((1, east), (2, west)):
                copy = remote(surf.at[0], surf.at[k], 5 + 4 * STEPS + k, (comp, lat, to))
                copy.start()
                surf_sends.append(copy)
        lo.wait_recv()
        hi.wait_recv()

        def unpack(offset):
            parts = []
            for g in range(groups):
                low, high = (
                    pltpu.roll(box[step], turn % cols, 1) if turn % cols else box[step]
                    for box, turn in ((from_lo, offset + 2 - g), (from_hi, offset + 1 - g))
                )
                parts.append(jnp.where(quad[:8] == 1, high, low))
            return jnp.concatenate(parts, axis=0)

        moved = unpack(0)
        signed = jnp.where(quad == 1, hp, -hp)
        u_side = unpack(cols - 4 * rows) + signed * packed
        u_fix = -signed * moved
        d_fix = jnp.where(
            quad == 1,
            u_side,
            jnp.where(
                quad == 2,
                -u_side,
                jnp.where(
                    quad == 0, pltpu.roll(u_fix, cols - 1, 1), -pltpu.roll(u_fix, 1, 1)
                ),
            ),
        )
        d_fix = hf * d_fix
        ends = first | last
        near = (lane < 2) | (lane > cols - 3)
        if step + 1 == STEPS:
            p_fix = -side_mask * jnp.dot(
                vert_cat, split(d_fix), preferred_element_type=jnp.float32
            )
            u_fix = side_mask * u_fix
            for y in range(rows):
                turn = cols - (4 * y + 2)
                for f, fix, where in ((0, u_fix, ends), (2, p_fix, near)):
                    at = pl.ds(f * plane + y, levels, stride=rows)
                    out[at, :] = out[at, :] + jnp.where(where, pltpu.roll(fix, turn, 1), 0.0)
            break
        p_side = jnp.dot(vert_cat, split(p_side - d_fix), preferred_element_type=jnp.float32)
        side = send_sides(
            step + 1,
            side_mask * p_side,
            side_mask * (u_edge + u_fix),
            side_mask * v_edge,
        )
        pieces = []
        for y in range(rows):
            turn = cols - (4 * y + 2)
            uone[y] = uone[y] + jnp.where(ends, pltpu.roll(u_fix, turn, 1), 0.0)
            p1 = pone[y] - jnp.where(near, pltpu.roll(d_fix, turn, 1), 0.0)
            pieces.append(split(p1))
        p2 = jnp.dot(
            vert_cat, jnp.concatenate(pieces, axis=1), preferred_element_type=jnp.float32
        )
        for y in range(rows):
            keep = mask[y : y + 1]
            unew[y] = keep * uone[y]
            vnew[y] = keep * vone[y]
            pres[y] = keep * p2[:, y * cols : (y + 1) * cols]

    for copy in sends + surf_sends:
        copy.wait_send()


def shards(n_lat, n_lon, state, push, fill, vertical, land, match, counts):
    _, fields, levels, rows, cols = state.shape
    assert fields == 3 and 8 * rows <= cols and levels % 8 == 0 and levels <= 32
    block = (rows, levels, cols)
    n_sems = 3 + 4 * STEPS + 5
    f32 = jnp.float32
    any_spec = pl.BlockSpec(memory_space=pl.ANY)
    result = pl.pallas_call(
        functools.partial(kernel, (levels, rows, cols, n_lat, n_lon)),
        out_shape=pltpu.VMEM((fields * levels * rows, cols), f32),
        in_specs=[any_spec] * 7,
        out_specs=pl.BlockSpec(memory_space=pltpu.VMEM),
        scratch_shapes=[
            pltpu.VMEM((fields * levels * rows, cols), f32),
            pltpu.VMEM(push.shape, f32),
            pltpu.VMEM(fill.shape, f32),
            pltpu.VMEM(vertical.shape[1:], f32),
            pltpu.VMEM(land.shape, jnp.int32),
            pltpu.VMEM(match.shape[:0:-1], jnp.int32),
            pltpu.VMEM(counts.shape[:0:-1], jnp.int32),
            pltpu.VMEM(block, f32),
            pltpu.VMEM(block, f32),
            pltpu.VMEM(block, f32),
            pltpu.VMEM(block, f32),
            pltpu.VMEM(block, f32),
            pltpu.VMEM(block, f32),
            pltpu.VMEM((STEPS, 2, 8, cols), f32),
            pltpu.VMEM((STEPS, 8, cols), f32),
            pltpu.VMEM((STEPS, 8, cols), f32),
            pltpu.VMEM((STEPS, 2, 2, levels, cols), f32),
            pltpu.VMEM((STEPS, 2, levels, cols), f32),
            pltpu.VMEM((STEPS, 2, levels, cols), f32),
            pltpu.VMEM((3, fields, rows, cols), f32),
            pltpu.SemaphoreType.DMA((9,)),
            pltpu.SemaphoreType.DMA((n_sems,)),
            pltpu.SemaphoreType.DMA((n_sems,)),
        ],
        compiler_params=pltpu.CompilerParams(collective_id=0, has_side_effects=True),
        name="window",
    )(
        state.reshape(fields * levels * rows, cols),
        push,
        fill,
        vertical.reshape(vertical.shape[1:]),
        land,
        match[0].T,
        counts[0].T,
    )
    return result.reshape(state.shape)


def solution(mesh):
    sizes = dict(mesh.shape)
    return jax.shard_map(
        functools.partial(shards, sizes["lat"], sizes["lon"]),
        mesh=mesh,
        in_specs=(
            P("comp", None, None, "lat", "lon"),
            P("comp", None),
            P("comp", None),
            P("comp", None, None),
            P("lat", "lon"),
            P("lat", None, None),
            P("lat", None, None),
        ),
        out_specs=P("comp", None, None, "lat", "lon"),
        check_vma=False,
    )
```
